32 devices in a mesh: child: 4 (over y, x), shard: 8 (over z, core).
Axes of the slice: x: 2, y: 2, z: 4, core: 2. Of those that a mesh axis runs over, the one named last changes fastest.
Arguments:
- child_tensors: bfloat16 [4, 256, 256, 256], P('child', 'shard'), may hold values from -6 to 6
- leg_ops: bfloat16 [8, 256, 256], replicated, may hold values from -0.375 to 0.375
- term_ops: int32 [4, 4, 2], P('child'), may hold values from 0 to 7
- term_coef: float32 [4, 4], P('child'), may hold values from 0.5 to 1.5
- parent: bfloat16 [4, 256, 256], P('child', 'shard'), may hold values from -0.375 to 0.375
- top_env: float32 [256, 256], replicated, may hold values from -6 to 6
Outputs:
- applied: bfloat16 [4, 256, 256, 256], P('child', None, 'shard')
The draws below stay inside these ranges and needn't reach their ends.
Inputs may be any that keep to these rules, and one draw needn't show every extreme that they name: `term_ops`: each entry names one of the 8 leg operators.
All inputs are finite; a program needn't handle non-finite values.
Results may differ from the reference program's by a relative error of at most 0.0091.
Values may be sent and summed in bfloat16 or wider, within the bound.
A program may use at most 128 MiB of HBM per device.

```python
import math
import jax
import jax.numpy as jnp
from jax import lax

B = 256
TPC = 4
NOPS = 8
CHILDREN = 4


def place_ends(array, own_key, least, high):
    place = [jax.random.randint(jax.random.fold_in(own_key, axis), (), 0, length) for axis, length in enumerate(array.shape)]
    widest = array.shape.index(max(array.shape))
    beside = place[:widest] + [(place[widest] + 1) % array.shape[widest]] + place[widest + 1:]
    return array.at[tuple(place)].set(least).at[tuple(beside)].set(high)


def level_of(key, extent, split, least, largest):
    gain = 1.0
    for axis_at, parts in split:
        steps = jax.random.uniform(jax.random.fold_in(jax.random.fold_in(key, 6), axis_at), (parts,), jnp.float32, least / len(split), largest / len(split))
        gain = gain * jnp.repeat(jnp.exp(steps), extent[axis_at] // parts).reshape((-1,) + (1,) * (len(extent) - 1 - axis_at))
    return gain


def gaussian(key, dims, spread, most, cuts=(), kind=jnp.bfloat16):
    result = spread * jax.random.normal(key, dims, jnp.float32)
    if cuts:
        result = result * level_of(key, dims, cuts, -0.22, 0.18)
    return jnp.clip(result, -most, most).astype(kind)


def setup_inputs(seed: int = 0) -> dict:
    streams_of = jax.random.split(jax.random.key(seed), 7)
    child_tensors = gaussian(streams_of[0], (CHILDREN, B, B, B), 1.0, 6.0, ((0, 4), (1, 8)))
    leg_ops = gaussian(streams_of[1], (NOPS, B, B), B ** -0.5, 0.375)
    term_ops = place_ends(jax.random.randint(streams_of[2], (CHILDREN, TPC, 2), 0, NOPS), jax.random.fold_in(streams_of[2], 1), 0, NOPS - 1).astype(jnp.int32)
    term_coef = jnp.clip(0.5 + 1.0 * jax.random.uniform(streams_of[3], (CHILDREN, TPC), jnp.float32) ** level_of(streams_of[3], (CHILDREN, TPC), ((0, 4),), -0.2, 0.2), 0.5, 1.5)
    parent = gaussian(streams_of[4], (CHILDREN, B, B), B ** -0.5, 0.375, ((0, 4), (1, 8)))
    top_env = gaussian(streams_of[5], (B, B), 1.0, 6.0, (), jnp.float32)
    return dict(child_tensors=child_tensors, leg_ops=leg_ops, term_ops=term_ops, term_coef=term_coef, parent=parent, top_env=top_env)


def reference(child_tensors, leg_ops, term_ops, term_coef, parent, top_env):
    high = lax.Precision.HIGHEST
    bank = leg_ops.astype(jnp.float32)

    def first(item):
        tensor, picks, weights, block = item
        dense = tensor.astype(jnp.float32)
        lift = block.astype(jnp.float32)
        local = jnp.zeros((B, B, B), jnp.float32)
        for term in range(TPC):
            right = bank[picks[term, 1]]
            left = bank[picks[term, 0]]
            image = jnp.einsum('lru,rs->lsu', dense, right, precision=high).astype(jnp.bfloat16)
            image = lax.optimization_barrier(image).astype(jnp.float32)
            local = local + weights[term] * jnp.einsum('lk,lsu->ksu', left, image, precision=high)
        rounded = lax.optimization_barrier(local.astype(jnp.bfloat16)).astype(jnp.float32)
        env = jnp.einsum('lsu,lsv->uv', dense, rounded, precision=high) / B
        lifted = jnp.dot(lift.T, jnp.dot(env, lift, precision=high), precision=high)
        return (local, lifted)
    locals_all, lifted_all = lax.map(first, (child_tensors, term_ops, term_coef, parent))
    total = lax.optimization_barrier(jnp.sum(lifted_all, axis=0))
    factor = 1.0 / math.sqrt(B * CHILDREN)

    def second(item):
        tensor, local, block, own = item
        lift = block.astype(jnp.float32)
        coupling = total - own + top_env
        hole = jnp.dot(jnp.dot(lift, coupling, precision=high), lift.T, precision=high) * factor
        hole = hole.astype(jnp.bfloat16).astype(jnp.float32)
        moved = jnp.einsum('lsu,uv->lsv', tensor.astype(jnp.float32), hole, precision=high)
        return (local + moved).astype(jnp.bfloat16)
    return lax.map(second, (child_tensors, locals_all, parent, lifted_all))
```

```python
import functools
import math

import jax
import jax.numpy as jnp
from jax import lax
from jax.experimental import pallas as pl
from jax.experimental.pallas import tpu as pltpu
from jax.sharding import PartitionSpec as P

MESH = pl.DeviceIdType.MESH
HIGH = lax.Precision.HIGHEST


def tail_kernel(
    n, nc, bond, factor, env_ref, par_ref, top_ref, hole_ref,
    parv, envv, envf, lif, chv, cpf, ssem, rsem,
):
    me = lax.axis_index("shard")
    kid = lax.axis_index("child")
    rows, width = env_ref.shape[1], env_ref.shape[2]
    peers = [lax.rem(me + k, n) for k in range(1, n)]
    kids = [lax.rem(kid + k, nc) for k in range(1, nc)]
    barrier = pltpu.get_barrier_semaphore()
    for j in peers:
        pl.semaphore_signal(barrier, inc=1, device_id={"shard": j}, device_id_type=MESH)
    for j in kids:
        pl.semaphore_signal(barrier, inc=1, device_id={"child": j}, device_id_type=MESH)
    pl.semaphore_wait(barrier, n + nc - 2)

    def send(phase, src, dst, axis, j, own):
        copy = pltpu.make_async_remote_copy(
            src_ref=src, dst_ref=dst, send_sem=ssem.at[phase, j], recv_sem=rsem.at[phase, own],
            device_id={axis: j}, device_id_type=MESH,
        )
        copy.start()
        return copy

    def arrive(phase, ref, axis, j):
        pltpu.make_async_remote_copy(
            src_ref=ref, dst_ref=ref, send_sem=ssem.at[phase, j], recv_sem=rsem.at[phase, j],
            device_id={axis: j}, device_id_type=MESH,
        ).wait_recv()

    sent = [send(0, env_ref.at[j], envv.at[me], "shard", j, me) for j in peers]
    sent += [send(1, par_ref, parv.at[me], "shard", j, me) for j in peers]
    parv[me] = par_ref[...]
    total = env_ref[me]
    for j in peers:
        arrive(0, envv.at[j], "shard", j)
        total = total + envv[j]
    envf[me] = total
    sent += [send(2, envf.at[me], envf.at[me], "shard", j, me) for j in peers]
    for j in peers:
        arrive(1, parv.at[j], "shard", j)
    lift = parv[...].astype(jnp.float32).reshape(n * rows, width)
    for j in peers:
        arrive(2, envf.at[j], "shard", j)
    env = envf[...].reshape(n * rows, width) * (1.0 / bond)
    half = jnp.dot(env, lift, precision=HIGH, preferred_element_type=jnp.float32)
    lifted = lax.dot_general(
        lift, half, (((0,), (0,)), ((), ())), precision=HIGH, preferred_element_type=jnp.float32
    )
    lif[...] = lifted.reshape(n, rows, width)
    sent += [send(3, lif.at[me], chv.at[kid], "child", j, kid) for j in kids]
    slab = top_ref[me]
    for j in kids:
        arrive(3, chv.at[j], "child", j)
        slab = slab + chv[j]
    cpf[me] = slab
    sent += [send(4, cpf.at[me], cpf.at[me], "shard", j, me) for j in peers]
    for j in peers:
        arrive(4, cpf.at[j], "shard", j)
    coupling = cpf[...].reshape(n * rows, width)
    half = jnp.dot(lift, coupling, precision=HIGH, preferred_element_type=jnp.float32)
    hole = lax.dot_general(
        half, lift, (((1,), (1,)), ((), ())), precision=HIGH, preferred_element_type=jnp.float32
    )
    hole_ref[...] = (hole * factor).astype(jnp.bfloat16)
    for copy in sent:
        copy.wait_send()


def hole_of(env_part, parent_block, top_env):
    n, nc = lax.axis_size("shard"), lax.axis_size("child")
    rows, width = parent_block.shape
    bond = env_part.shape[0]
    factor = 1.0 / math.sqrt(bond * nc)
    most = max(n, nc)
    vmem = pl.BlockSpec(memory_space=pltpu.VMEM)
    block = lambda count, kind: pltpu.VMEM((count, rows, width), kind)
    return pl.pallas_call(
        functools.partial(tail_kernel, n, nc, bond, factor),
        out_shape=jax.ShapeDtypeStruct((bond, bond), jnp.bfloat16),
        in_specs=[vmem] * 3,
        out_specs=vmem,
        scratch_shapes=[
            block(n, jnp.bfloat16),
            block(n, jnp.float32),
            block(n, jnp.float32),
            block(n, jnp.float32),
            block(nc, jnp.float32),
            block(n, jnp.float32),
            pltpu.SemaphoreType.DMA((5, most)),
            pltpu.SemaphoreType.DMA((5, most)),
        ],
        compiler_params=pltpu.CompilerParams(collective_id=0, has_side_effects=True),
    )(env_part.reshape(n, rows, bond), parent_block, top_env.reshape(n, rows, width))


def shards(child_tensors, leg_ops, term_ops, term_coef, parent, top_env):
    tensor = child_tensors[0]
    bond = tensor.shape[1]
    picks = term_ops[0]
    weights = term_coef[0]
    number = weights.shape[0]
    left_ops = leg_ops[picks[:, 0]]
    right_ops = leg_ops[picks[:, 1]]
    upward = lax.all_to_all(tensor, "shard", split_axis=2, concat_axis=0, tiled=True)
    regrouped = lax.all_to_all(tensor, "shard", split_axis=1, concat_axis=0, tiled=True)
    summed = jnp.zeros((bond, bond, upward.shape[2]), jnp.float32)
    for term in range(number):
        image = jnp.einsum(
            "lru,rs->lsu", upward, right_ops[term], preferred_element_type=jnp.float32
        ).astype(jnp.bfloat16)
        summed = summed + weights[term] * jnp.einsum(
            "lk,lsu->ksu", left_ops[term], image, preferred_element_type=jnp.float32
        )
    local = lax.all_to_all(
        summed.astype(jnp.bfloat16), "shard", split_axis=1, concat_axis=2, tiled=True
    )
    env_part = jnp.einsum("lsu,lsv->uv", regrouped, local, preferred_element_type=jnp.float32)
    hole = hole_of(env_part, parent[0], top_env)
    result = local.astype(jnp.float32) + jnp.einsum(
        "lsu,uv->lsv", regrouped, hole, preferred_element_type=jnp.float32
    )
    return result.astype(jnp.bfloat16)[None]


def solution(mesh):
    in_specs = (
        P("child", "shard", None, None),
        P(),
        P("child", None, None),
        P("child", None),
        P("child", "shard", None),
        P(),
    )
    out_specs = P("child", None, "shard", None)
    return jax.shard_map(shards, mesh=mesh, in_specs=in_specs, out_specs=out_specs, check_vma=False)
```

```python
import functools
import math

import jax
import jax.numpy as jnp
from jax import lax
from jax.experimental import pallas as pl
from jax.experimental.pallas import tpu as pltpu
from jax.sharding import PartitionSpec as P

MESH = pl.DeviceIdType.MESH
HIGH = lax.Precision.HIGHEST


def tail_kernel(
    n, nc, bond, factor, env_ref, par_ref, top_ref, hole_ref,
    parv, envv, envf, lif, chv, cpf, ssem, rsem,
):
    me = lax.axis_index("shard")
    kid = lax.axis_index("child")
    rows, width = env_ref.shape[1], env_ref.shape[2]
    peers = [lax.rem(me + k, n) for k in range(1, n)]
    kids = [lax.rem(kid + k, nc) for k in range(1, nc)]
    barrier = pltpu.get_barrier_semaphore()
    for j in peers:
        pl.semaphore_signal(barrier, inc=1, device_id={"shard": j}, device_id_type=MESH)
    for j in kids:
        pl.semaphore_signal(barrier, inc=1, device_id={"child": j}, device_id_type=MESH)
    pl.semaphore_wait(barrier, n + nc - 2)

    def send(phase, src, dst, axis, j, own):
        copy = pltpu.make_async_remote_copy(
            src_ref=src, dst_ref=dst, send_sem=ssem.at[phase, j], recv_sem=rsem.at[phase, own],
            device_id={axis: j}, device_id_type=MESH,
        )
        copy.start()
        return copy

    def arrive(phase, ref, axis, j):
        pltpu.make_async_remote_copy(
            src_ref=ref, dst_ref=ref, send_sem=ssem.at[phase, j], recv_sem=rsem.at[phase, j],
            device_id={axis: j}, device_id_type=MESH,
        ).wait_recv()

    sent = [send(0, env_ref.at[j], envv.at[me], "shard", j, me) for j in peers]
    sent += [send(1, par_ref, parv.at[me], "shard", j, me) for j in peers]
    parv[me] = par_ref[...]
    total = env_ref[me]
    for j in peers:
        arrive(0, envv.at[j], "shard", j)
        total = total + envv[j]
    envf[me] = total
    sent += [send(2, envf.at[me], envf.at[me], "shard", j, me) for j in peers]
    for j in peers:
        arrive(1, parv.at[j], "shard", j)
    lift = parv[...].astype(jnp.float32).reshape(n * rows, width)
    for j in peers:
        arrive(2, envf.at[j], "shard", j)
    env = envf[...].reshape(n * rows, width) * (1.0 / bond)
    half = jnp.dot(env, lift, precision=HIGH, preferred_element_type=jnp.float32)
    lifted = lax.dot_general(
        lift, half, (((0,), (0,)), ((), ())), precision=HIGH, preferred_element_type=jnp.float32
    )
    lif[...] = lifted.reshape(n, rows, width)
    sent += [send(3, lif.at[me], chv.at[kid], "child", j, kid) for j in kids]
    slab = top_ref[me]
    for j in kids:
        arrive(3, chv.at[j], "child", j)
        slab = slab + chv[j]
    cpf[me] = slab
    sent += [send(4, cpf.at[me], cpf.at[me], "shard", j, me) for j in peers]
    for j in peers:
        arrive(4, cpf.at[j], "shard", j)
    coupling = cpf[...].reshape(n * rows, width)
    half = jnp.dot(lift, coupling, precision=HIGH, preferred_element_type=jnp.float32)
    hole = lax.dot_general(
        half, lift, (((1,), (1,)), ((), ())), precision=HIGH, preferred_element_type=jnp.float32
    )
    hole_ref[...] = (hole * factor).astype(jnp.bfloat16)
    for copy in sent:
        copy.wait_send()


def hole_of(env_part, parent_block, top_env):
    n, nc = lax.axis_size("shard"), lax.axis_size("child")
    rows, width = parent_block.shape
    bond = env_part.shape[0]
    factor = 1.0 / math.sqrt(bond * nc)
    most = max(n, nc)
    vmem = pl.BlockSpec(memory_space=pltpu.VMEM)
    block = lambda count, kind: pltpu.VMEM((count, rows, width), kind)
    return pl.pallas_call(
        functools.partial(tail_kernel, n, nc, bond, factor),
        out_shape=jax.ShapeDtypeStruct((bond, bond), jnp.bfloat16),
        in_specs=[vmem] * 3,
        out_specs=vmem,
        scratch_shapes=[
            block(n, jnp.bfloat16),
            block(n, jnp.float32),
            block(n, jnp.float32),
            block(n, jnp.float32),
            block(nc, jnp.float32),
            block(n, jnp.float32),
            pltpu.SemaphoreType.DMA((5, most)),
            pltpu.SemaphoreType.DMA((5, most)),
        ],
        compiler_params=pltpu.CompilerParams(collective_id=0, has_side_effects=True),
    )(env_part.reshape(n, rows, bond), parent_block, top_env.reshape(n, rows, width))


CHUNK = 32
GROUP = 8


def core_kernel(
    n, number, tens_ref, rc_ref, coef_ref, left_ref, tsel_ref, loc_ref,
    full, image, stage_t, stage_l, own_sem, ssem, fsem, esem, rsem, xsem,
):
    me = lax.axis_index("shard")
    cores = 2
    chips = n // cores
    chip, core = me // cores, lax.rem(me, cores)
    rows = tens_ref.shape[1]
    half = full.shape[0]
    steps = half // CHUNK
    side = lax.rem(chip, 2)
    twin = chip * cores + 1 - core
    mate = (chip + 1 - 2 * side) * cores + core
    others = [lax.rem(chip + k, chips) for k in range(1, chips)]

    barrier = pltpu.get_barrier_semaphore()
    for k in range(1, n):
        pl.semaphore_signal(
            barrier, inc=1, device_id={"shard": lax.rem(me + k, n)}, device_id_type=MESH
        )
    pl.semaphore_wait(barrier, n - 1)

    def place(q, j):
        return full.at[pl.ds(q * CHUNK, CHUNK), pl.ds(pl.multiple_of(j * rows, rows), rows), :]

    def source(q, which):
        return tens_ref.at[pl.ds(which * half + q * CHUNK, CHUNK)]

    def remote(src, dst, send, recv, j):
        return pltpu.make_async_remote_copy(
            src_ref=src, dst_ref=dst, send_sem=send, recv_sem=recv,
            device_id={"shard": j}, device_id_type=MESH,
        )

    sent = []
    local_copies = []
    for q in range(steps):
        for z in others:
            copy = remote(
                source(q, lax.rem(z, 2)), place(q, me), ssem.at[q, z], rsem.at[q, me],
                z * cores + core,
            )
            copy.start()
            sent.append(copy)
        copy = remote(source(q, side), place(q, me), fsem.at[q, chip], rsem.at[q, me], twin)
        copy.start()
        sent.append(copy)
        copy = pltpu.make_async_copy(source(q, side), place(q, me), own_sem.at[q])
        copy.start()
        local_copies.append(copy)

    for q in range(steps):
        for z in others:
            j = z * cores + core
            remote(place(q, j), place(q, j), ssem.at[q, z], rsem.at[q, j], twin).wait_recv()
            copy = remote(place(q, j), place(q, j), fsem.at[q, z], rsem.at[q, j], twin)
            copy.start()
            sent.append(copy)
        local_copies[q].wait()
        for z in [chip] + others:
            j = z * cores + 1 - core
            remote(place(q, j), place(q, j), fsem.at[q, z], rsem.at[q, j], twin).wait_recv()

        def block(g, _):
            first = q * CHUNK + g * GROUP
            goal = side * half + first
            for i in range(GROUP):
                made = lax.dot_general(
                    rc_ref[...], full[first + i], (((1,), (1,)), ((), ())),
                    preferred_element_type=jnp.float32,
                )
                made = (made * coef_ref[...]).astype(jnp.bfloat16)
                for t in range(number):
                    image[t, pl.ds(i * 2 * rows, 2 * rows), :] = made[
                        t * 2 * rows : (t + 1) * 2 * rows
                    ]
                base = number * 2 * rows
                tsel_ref[goal + i] = made[base : base + rows]
                stage_t[first + i] = made[base + rows : base + 2 * rows]
            total = jnp.dot(image[0], left_ref[0], preferred_element_type=jnp.float32)
            for t in range(1, number):
                total += jnp.dot(image[t], left_ref[t], preferred_element_type=jnp.float32)
            total = total.astype(jnp.bfloat16).reshape(GROUP, 2 * rows, total.shape[-1])
            loc_ref[pl.ds(goal, GROUP)] = total[:, :rows]
            stage_l[pl.ds(first, GROUP)] = total[:, rows:]
            return 0

        lax.fori_loop(0, CHUNK // GROUP, block, 0)
        here = pl.ds(q * CHUNK, CHUNK)
        there = pl.ds(side * half + q * CHUNK, CHUNK)
        for which, (stage, goal_ref) in enumerate(((stage_t, tsel_ref), (stage_l, loc_ref))):
            copy = remote(
                stage.at[here], goal_ref.at[there], esem.at[which, q], xsem.at[which, q], mate
            )
            copy.start()
            sent.append(copy)
    for q in range(steps):
        far = pl.ds((1 - side) * half + q * CHUNK, CHUNK)
        for which, goal_ref in enumerate((tsel_ref, loc_ref)):
            remote(
                goal_ref.at[far], goal_ref.at[far], esem.at[which, q], xsem.at[which, q], mate
            ).wait_recv()
    for copy in sent:
        copy.wait_send()


def local_of(tensor, left_ops, right_ops, weights):
    n = lax.axis_size("shard")
    me = lax.axis_index("shard")
    rows, bond = tensor.shape[0], tensor.shape[1]
    number = weights.shape[0]
    half = bond // 2
    steps = half // CHUNK
    chip = me // 2
    mate = (chip + 1 - 2 * (chip % 2)) * 2 + me % 2
    pair = jnp.stack([me, mate])
    slabs = jnp.swapaxes(right_ops, 1, 2).reshape(number, n, rows, bond)
    chosen = slabs[:, pair]
    wanted = pair[:, None] * rows + jnp.arange(rows)[None, :]
    onehot = (wanted[:, :, None] == jnp.arange(bond)).astype(jnp.bfloat16)
    rc = jnp.concatenate([chosen, onehot[None]], axis=0).reshape((number + 1) * 2 * rows, bond)
    coef = jnp.repeat(jnp.concatenate([weights, jnp.ones((1,), jnp.float32)]), 2 * rows)[:, None]
    upward = jnp.transpose(tensor, (2, 0, 1))
    vmem = pl.BlockSpec(memory_space=pltpu.VMEM)
    hbm = pl.BlockSpec(memory_space=pl.ANY)
    slab = jax.ShapeDtypeStruct((bond, rows, bond), jnp.bfloat16)
    dma = pltpu.SemaphoreType.DMA
    return pl.pallas_call(
        functools.partial(core_kernel, n, number),
        out_shape=(slab, slab),
        in_specs=[hbm, vmem, vmem, vmem],
        out_specs=(vmem, vmem),
        scratch_shapes=[
            pltpu.VMEM((half, bond, bond), jnp.bfloat16),
            pltpu.VMEM((number, GROUP * 2 * rows, bond), jnp.bfloat16),
            pltpu.VMEM((half, rows, bond), jnp.bfloat16),
            pltpu.VMEM((half, rows, bond), jnp.bfloat16),
            dma((steps,)),
            dma((steps, n // 2)),
            dma((steps, n // 2)),
            dma((2, steps)),
            dma((steps, n)),
            dma((2, steps)),
        ],
        compiler_params=pltpu.CompilerParams(
            collective_id=1, has_side_effects=True, vmem_limit_bytes=56 * 1024 * 1024
        ),
    )(upward, rc, coef, left_ops)


def by_exchange(tensor, left_ops, right_ops, weights):
    bond = tensor.shape[1]
    upward = lax.all_to_all(tensor, "shard", split_axis=2, concat_axis=0, tiled=True)
    regrouped = lax.all_to_all(tensor, "shard", split_axis=1, concat_axis=0, tiled=True)
    summed = jnp.zeros((bond, bond, upward.shape[2]), jnp.float32)
    for term in range(weights.shape[0]):
        image = jnp.einsum(
            "lru,rs->lsu", upward, right_ops[term], preferred_element_type=jnp.float32
        ).astype(jnp.bfloat16)
        summed = summed + weights[term] * jnp.einsum(
            "lk,lsu->ksu", left_ops[term], image, preferred_element_type=jnp.float32
        )
    local = lax.all_to_all(
        summed.astype(jnp.bfloat16), "shard", split_axis=1, concat_axis=2, tiled=True
    )
    return jnp.transpose(regrouped, (2, 1, 0)), jnp.transpose(local, (2, 1, 0))


def shards(child_tensors, leg_ops, term_ops, term_coef, parent, top_env):
    tensor = child_tensors[0]
    picks = term_ops[0]
    weights = term_coef[0]
    left_ops = leg_ops[picks[:, 0]]
    right_ops = leg_ops[picks[:, 1]]
    form = local_of if tensor.shape[0] % 16 == 0 else by_exchange
    slab, local = form(tensor, left_ops, right_ops, weights)
    env_part = jnp.einsum("usl,vsl->uv", slab, local, preferred_element_type=jnp.float32)
    hole = hole_of(env_part, parent[0], top_env)
    result = jnp.transpose(local, (2, 1, 0)).astype(jnp.float32) + jnp.einsum(
        "usl,uv->lsv", slab, hole, preferred_element_type=jnp.float32
    )
    return result.astype(jnp.bfloat16)[None]


def solution(mesh):
    in_specs = (
        P("child", "shard", None, None),
        P(),
        P("child", None, None),
        P("child", None),
        P("child", "shard", None),
        P(),
    )
    out_specs = P("child", None, "shard", None)
    return jax.shard_map(shards, mesh=mesh, in_specs=in_specs, out_specs=out_specs, check_vma=False)
```

```python
import functools
import math

import jax
import jax.numpy as jnp
from jax import lax
from jax.experimental import pallas as pl
from jax.experimental.pallas import tpu as pltpu
from jax.sharding import PartitionSpec as P

MESH = pl.DeviceIdType.MESH
HIGH = lax.Precision.HIGHEST


def tail_kernel(
    n, nc, bond, factor, env_ref, par_ref, top_ref, hole_ref,
    parv, envv, envf, lif, chv, cpf, ssem, rsem,
):
    me = lax.axis_index("shard")
    kid = lax.axis_index("child")
    rows, width = env_ref.shape[1], env_ref.shape[2]
    peers = [lax.rem(me + k, n) for k in range(1, n)]
    kids = [lax.rem(kid + k, nc) for k in range(1, nc)]
    barrier = pltpu.get_barrier_semaphore()
    for j in peers:
        pl.semaphore_signal(barrier, inc=1, device_id={"shard": j}, device_id_type=MESH)
    for j in kids:
        pl.semaphore_signal(barrier, inc=1, device_id={"child": j}, device_id_type=MESH)
    pl.semaphore_wait(barrier, n + nc - 2)

    def send(phase, src, dst, axis, j, own):
        copy = pltpu.make_async_remote_copy(
            src_ref=src, dst_ref=dst, send_sem=ssem.at[phase, j], recv_sem=rsem.at[phase, own],
            device_id={axis: j}, device_id_type=MESH,
        )
        copy.start()
        return copy

    def arrive(phase, ref, axis, j):
        pltpu.make_async_remote_copy(
            src_ref=ref, dst_ref=ref, send_sem=ssem.at[phase, j], recv_sem=rsem.at[phase, j],
            device_id={axis: j}, device_id_type=MESH,
        ).wait_recv()

    sent = [send(0, env_ref.at[j], envv.at[me], "shard", j, me) for j in peers]
    sent += [send(1, par_ref, parv.at[me], "shard", j, me) for j in peers]
    parv[me] = par_ref[...]
    total = env_ref[me].astype(jnp.float32)
    for j in peers:
        arrive(0, envv.at[j], "shard", j)
        total = total + envv[j].astype(jnp.float32)
    envf[me] = total.astype(jnp.bfloat16)
    sent += [send(2, envf.at[me], envf.at[me], "shard", j, me) for j in peers]
    for j in peers:
        arrive(1, parv.at[j], "shard", j)
    lift = parv[...].astype(jnp.float32).reshape(n * rows, width)
    for j in peers:
        arrive(2, envf.at[j], "shard", j)
    env = envf[...].astype(jnp.float32).reshape(n * rows, width) * (1.0 / bond)
    half = jnp.dot(env, lift, precision=HIGH, preferred_element_type=jnp.float32)
    lifted = lax.dot_general(
        lift, half, (((0,), (0,)), ((), ())), precision=HIGH, preferred_element_type=jnp.float32
    )
    lif[...] = lifted.reshape(n, rows, width)
    sent += [send(3, lif.at[me], chv.at[kid], "child", j, kid) for j in kids]
    slab = top_ref[me]
    for j in kids:
        arrive(3, chv.at[j], "child", j)
        slab = slab + chv[j]
    cpf[me] = slab.astype(jnp.bfloat16)
    sent += [send(4, cpf.at[me], cpf.at[me], "shard", j, me) for j in peers]
    for j in peers:
        arrive(4, cpf.at[j], "shard", j)
    coupling = cpf[...].astype(jnp.float32).reshape(n * rows, width)
    half = jnp.dot(lift, coupling, precision=HIGH, preferred_element_type=jnp.float32)
    hole = lax.dot_general(
        half, lift, (((1,), (1,)), ((), ())), precision=HIGH, preferred_element_type=jnp.float32
    )
    hole_ref[...] = (hole * factor).astype(jnp.bfloat16)
    for copy in sent:
        copy.wait_send()


def hole_of(env_part, parent_block, top_env):
    n, nc = lax.axis_size("shard"), lax.axis_size("child")
    rows, width = parent_block.shape
    bond = env_part.shape[0]
    factor = 1.0 / math.sqrt(bond * nc)
    most = max(n, nc)
    vmem = pl.BlockSpec(memory_space=pltpu.VMEM)
    block = lambda count, kind: pltpu.VMEM((count, rows, width), kind)
    return pl.pallas_call(
        functools.partial(tail_kernel, n, nc, bond, factor),
        out_shape=jax.ShapeDtypeStruct((bond, bond), jnp.bfloat16),
        in_specs=[vmem] * 3,
        out_specs=vmem,
        scratch_shapes=[
            block(n, jnp.bfloat16),
            block(n, jnp.bfloat16),
            block(n, jnp.bfloat16),
            block(n, jnp.float32),
            block(nc, jnp.float32),
            block(n, jnp.bfloat16),
            pltpu.SemaphoreType.DMA((5, most)),
            pltpu.SemaphoreType.DMA((5, most)),
        ],
        compiler_params=pltpu.CompilerParams(collective_id=0, has_side_effects=True),
    )(env_part.astype(jnp.bfloat16).reshape(n, rows, bond), parent_block, top_env.reshape(n, rows, width))


CHUNK = 16
GROUP = 8
LINE = 4


def core_kernel(
    n, number, tens_ref, rc_ref, coef_ref, left_ref, tsel_ref, loc_ref,
    full, image, stage_t, stage_l, own_sem, csem, fsem, esem, rsem, xsem,
):
    me = lax.axis_index("shard")
    cores = n // LINE
    chip, core = me // cores, lax.rem(me, cores)
    rows = tens_ref.shape[1]
    steps = tens_ref.shape[0] // CHUNK
    other = 1 - core
    mate_chip = chip + 1 - 2 * lax.rem(chip, 2)
    twin = chip * cores + other
    mate = mate_chip * cores + core
    across = (LINE - 1 - chip) * cores + core
    far = (LINE - 1 - mate_chip) * cores + core
    middle = jnp.logical_or(chip == 1, chip == 2)
    edge = jnp.logical_or(chip == 0, chip == 3)

    barrier = pltpu.get_barrier_semaphore()
    for k in range(1, n):
        pl.semaphore_signal(
            barrier, inc=1, device_id={"shard": lax.rem(me + k, n)}, device_id_type=MESH
        )
    pl.semaphore_wait(barrier, n - 1)

    def span(q):
        return pl.ds(pl.multiple_of(q * CHUNK, CHUNK), CHUNK)

    def place(q, j):
        return full.at[span(q), pl.ds(pl.multiple_of(j * rows, rows), rows), :]

    def remote(src, dst, send, recv, j):
        return pltpu.make_async_remote_copy(
            src_ref=src, dst_ref=dst, send_sem=send, recv_sem=recv,
            device_id={"shard": j}, device_id_type=MESH,
        )

    def own_to(q, send, j):
        return remote(tens_ref.at[span(q)], place(q, me), send, rsem.at[q, me], j)

    def pass_on(q, j, send, goal):
        return remote(place(q, j), place(q, j), send, rsem.at[q, j], goal)

    def finished(which, q):
        stage, goal_ref = ((stage_t, tsel_ref), (stage_l, loc_ref))[which]
        return remote(
            stage.at[span(q)], goal_ref.at[span(q)], esem.at[which, q], xsem.at[which, q], mate
        )

    def kept(q):
        return pltpu.make_async_copy(tens_ref.at[span(q)], place(q, me), own_sem.at[q])

    def loop(count, body):
        def step(q, _):
            body(q)
            return 0

        lax.fori_loop(0, count, step, 0)

    @pl.when(edge)
    def _():
        loop(steps, lambda q: own_to(q, csem.at[0, q], mate).start())

        def take(q):
            own_to(q, csem.at[0, q], mate).wait_send()
            for which in range(2):
                finished(which, q).wait_recv()

        loop(steps, take)

    @pl.when(middle)
    def _():
        def begin(q):
            own_to(q, fsem.at[0, q], twin).start()
            kept(q).start()

        loop(steps, begin)

        def relay(q):
            own_to(q, csem.at[0, q], across).start()
            pass_on(q, mate, csem.at[1, q], twin).wait_recv()
            pass_on(q, mate, csem.at[1, q], across).start()
            pass_on(q, mate, fsem.at[1, q], twin).start()

        relay(0)
        relay(1)

        def chunk(q):
            @pl.when(q + 2 < steps)
            def _():
                relay(q + 2)

            for slot, j in ((2, across), (3, far)):
                pass_on(q, j, fsem.at[slot, q], twin).wait_recv()
                pass_on(q, j, fsem.at[slot, q], twin).start()
            kept(q).wait()
            for slot, j in enumerate((me, mate, across, far)):
                pass_on(q, j + other - core, fsem.at[slot, q], twin).wait_recv()

            def block(g, _):
                first = q * CHUNK + g * GROUP
                for i in range(GROUP):
                    made = lax.dot_general(
                        rc_ref[...], full[first + i], (((1,), (1,)), ((), ())),
                        preferred_element_type=jnp.float32,
                    )
                    made = (made * coef_ref[...]).astype(jnp.bfloat16)
                    for t in range(number):
                        image[t, pl.ds(i * 2 * rows, 2 * rows), :] = made[
                            t * 2 * rows : (t + 1) * 2 * rows
                        ]
                    base = number * 2 * rows
                    tsel_ref[first + i] = made[base : base + rows]
                    stage_t[first + i] = made[base + rows : base + 2 * rows]
                total = jnp.dot(image[0], left_ref[0], preferred_element_type=jnp.float32)
                for t in range(1, number):
                    total += jnp.dot(image[t], left_ref[t], preferred_element_type=jnp.float32)
                total = total.astype(jnp.bfloat16).reshape(GROUP, 2 * rows, total.shape[-1])
                loc_ref[pl.ds(first, GROUP)] = total[:, :rows]
                stage_l[pl.ds(first, GROUP)] = total[:, rows:]
                return 0

            lax.fori_loop(0, CHUNK // GROUP, block, 0)
            for which in range(2):
                finished(which, q).start()

        loop(steps, chunk)

        def drain(q):
            own_to(q, fsem.at[0, q], twin).wait_send()
            own_to(q, csem.at[0, q], across).wait_send()
            pass_on(q, mate, csem.at[1, q], across).wait_send()
            for slot, j in ((1, mate), (2, across), (3, far)):
                pass_on(q, j, fsem.at[slot, q], twin).wait_send()
            for which in range(2):
                finished(which, q).wait_send()

        loop(steps, drain)


def local_of(tensor, left_ops, right_ops, weights):
    n = lax.axis_size("shard")
    me = lax.axis_index("shard")
    rows, bond = tensor.shape[0], tensor.shape[1]
    number = weights.shape[0]
    steps = bond // CHUNK
    cores = n // LINE
    chip = me // cores
    mate = (chip + 1 - 2 * (chip % 2)) * cores + me % cores
    pair = jnp.stack([me, mate])
    slabs = jnp.swapaxes(right_ops, 1, 2).reshape(number, n, rows, bond)
    chosen = slabs[:, pair]
    wanted = pair[:, None] * rows + jnp.arange(rows)[None, :]
    onehot = (wanted[:, :, None] == jnp.arange(bond)).astype(jnp.bfloat16)
    rc = jnp.concatenate([chosen, onehot[None]], axis=0).reshape((number + 1) * 2 * rows, bond)
    coef = jnp.repeat(jnp.concatenate([weights, jnp.ones((1,), jnp.float32)]), 2 * rows)[:, None]
    upward = jnp.transpose(tensor, (2, 0, 1))
    vmem = pl.BlockSpec(memory_space=pltpu.VMEM)
    hbm = pl.BlockSpec(memory_space=pl.ANY)
    slab = jax.ShapeDtypeStruct((bond, rows, bond), jnp.bfloat16)
    dma = pltpu.SemaphoreType.DMA
    return pl.pallas_call(
        functools.partial(core_kernel, n, number),
        out_shape=(slab, slab),
        in_specs=[hbm, vmem, vmem, vmem],
        out_specs=(vmem, vmem),
        scratch_shapes=[
            pltpu.VMEM((bond, bond, bond), jnp.bfloat16),
            pltpu.VMEM((number, GROUP * 2 * rows, bond), jnp.bfloat16),
            pltpu.VMEM((bond, rows, bond), jnp.bfloat16),
            pltpu.VMEM((bond, rows, bond), jnp.bfloat16),
            dma((steps,)),
            dma((2, steps)),
            dma((4, steps)),
            dma((2, steps)),
            dma((steps, n)),
            dma((2, steps)),
        ],
        compiler_params=pltpu.CompilerParams(
            collective_id=1, has_side_effects=True, vmem_limit_bytes=60 * 1024 * 1024
        ),
    )(upward, rc, coef, left_ops)


def by_exchange(tensor, left_ops, right_ops, weights):
    bond = tensor.shape[1]
    upward = lax.all_to_all(tensor, "shard", split_axis=2, concat_axis=0, tiled=True)
    regrouped = lax.all_to_all(tensor, "shard", split_axis=1, concat_axis=0, tiled=True)
    summed = jnp.zeros((bond, bond, upward.shape[2]), jnp.float32)
    for term in range(weights.shape[0]):
        image = jnp.einsum(
            "lru,rs->lsu", upward, right_ops[term], preferred_element_type=jnp.float32
        ).astype(jnp.bfloat16)
        summed = summed + weights[term] * jnp.einsum(
            "lk,lsu->ksu", left_ops[term], image, preferred_element_type=jnp.float32
        )
    local = lax.all_to_all(
        summed.astype(jnp.bfloat16), "shard", split_axis=1, concat_axis=2, tiled=True
    )
    return jnp.transpose(regrouped, (2, 1, 0)), jnp.transpose(local, (2, 1, 0))


def shards(child_tensors, leg_ops, term_ops, term_coef, parent, top_env):
    tensor = child_tensors[0]
    picks = term_ops[0]
    weights = term_coef[0]
    left_ops = leg_ops[picks[:, 0]]
    right_ops = leg_ops[picks[:, 1]]
    form = local_of if lax.axis_size("shard") == 2 * LINE else by_exchange
    slab, local = form(tensor, left_ops, right_ops, weights)
    env_part = jnp.einsum("usl,vsl->uv", slab, local, preferred_element_type=jnp.float32)
    hole = hole_of(env_part, parent[0], top_env)
    result = jnp.transpose(local, (2, 1, 0)).astype(jnp.float32) + jnp.einsum(
        "usl,uv->lsv", slab, hole, preferred_element_type=jnp.float32
    )
    return result.astype(jnp.bfloat16)[None]


def solution(mesh):
    in_specs = (
        P("child", "shard", None, None),
        P(),
        P("child", None, None),
        P("child", None),
        P("child", "shard", None),
        P(),
    )
    out_specs = P("child", None, "shard", None)
    return jax.shard_map(shards, mesh=mesh, in_specs=in_specs, out_specs=out_specs, check_vma=False)
```

```python
import functools
import math

import jax
import jax.numpy as jnp
from jax import lax
from jax.experimental import pallas as pl
from jax.experimental.pallas import tpu as pltpu
from jax.sharding import PartitionSpec as P

MESH = pl.DeviceIdType.MESH
HIGH = lax.Precision.HIGHEST


def tail_kernel(
    n, nc, bond, factor, env_ref, par_ref, top_ref, hole_ref,
    parv, envv, envf, lif, chv, cpf, ssem, rsem,
):
    me = lax.axis_index("shard")
    kid = lax.axis_index("child")
    rows, width = env_ref.shape[1], env_ref.shape[2]
    peers = [lax.rem(me + k, n) for k in range(1, n)]
    kids = [lax.rem(kid + k, nc) for k in range(1, nc)]
    barrier = pltpu.get_barrier_semaphore()
    for j in peers:
        pl.semaphore_signal(barrier, inc=1, device_id={"shard": j}, device_id_type=MESH)
    for j in kids:
        pl.semaphore_signal(barrier, inc=1, device_id={"child": j}, device_id_type=MESH)
    pl.semaphore_wait(barrier, n + nc - 2)

    def send(phase, src, dst, axis, j, own):
        copy = pltpu.make_async_remote_copy(
            src_ref=src, dst_ref=dst, send_sem=ssem.at[phase, j], recv_sem=rsem.at[phase, own],
            device_id={axis: j}, device_id_type=MESH,
        )
        copy.start()
        return copy

    def arrive(phase, ref, axis, j):
        pltpu.make_async_remote_copy(
            src_ref=ref, dst_ref=ref, send_sem=ssem.at[phase, j], recv_sem=rsem.at[phase, j],
            device_id={axis: j}, device_id_type=MESH,
        ).wait_recv()

    sent = [send(0, env_ref.at[j], envv.at[me], "shard", j, me) for j in peers]
    sent += [send(1, par_ref, parv.at[me], "shard", j, me) for j in peers]
    parv[me] = par_ref[...]
    total = env_ref[me].astype(jnp.float32)
    for j in peers:
        arrive(0, envv.at[j], "shard", j)
        total = total + envv[j].astype(jnp.float32)
    envf[me] = total.astype(jnp.bfloat16)
    sent += [send(2, envf.at[me], envf.at[me], "shard", j, me) for j in peers]
    for j in peers:
        arrive(1, parv.at[j], "shard", j)
    lift = parv[...].astype(jnp.float32).reshape(n * rows, width)
    for j in peers:
        arrive(2, envf.at[j], "shard", j)
    env = envf[...].astype(jnp.float32).reshape(n * rows, width) * (1.0 / bond)
    half = jnp.dot(env, lift, precision=HIGH, preferred_element_type=jnp.float32)
    lifted = lax.dot_general(
        lift, half, (((0,), (0,)), ((), ())), precision=HIGH, preferred_element_type=jnp.float32
    )
    lif[...] = lifted.reshape(n, rows, width)
    sent += [send(3, lif.at[me], chv.at[kid], "child", j, kid) for j in kids]
    slab = top_ref[me]
    for j in kids:
        arrive(3, chv.at[j], "child", j)
        slab = slab + chv[j]
    cpf[me] = slab.astype(jnp.bfloat16)
    sent += [send(4, cpf.at[me], cpf.at[me], "shard", j, me) for j in peers]
    for j in peers:
        arrive(4, cpf.at[j], "shard", j)
    coupling = cpf[...].astype(jnp.float32).reshape(n * rows, width)
    half = jnp.dot(lift, coupling, precision=HIGH, preferred_element_type=jnp.float32)
    hole = lax.dot_general(
        half, lift, (((1,), (1,)), ((), ())), precision=HIGH, preferred_element_type=jnp.float32
    )
    hole_ref[...] = (hole * factor).astype(jnp.bfloat16)
    for copy in sent:
        copy.wait_send()


def hole_of(env_part, parent_block, top_env):
    n, nc = lax.axis_size("shard"), lax.axis_size("child")
    rows, width = parent_block.shape
    bond = env_part.shape[0]
    factor = 1.0 / math.sqrt(bond * nc)
    most = max(n, nc)
    vmem = pl.BlockSpec(memory_space=pltpu.VMEM)
    block = lambda count, kind: pltpu.VMEM((count, rows, width), kind)
    return pl.pallas_call(
        functools.partial(tail_kernel, n, nc, bond, factor),
        out_shape=jax.ShapeDtypeStruct((bond, bond), jnp.bfloat16),
        in_specs=[vmem] * 3,
        out_specs=vmem,
        scratch_shapes=[
            block(n, jnp.bfloat16),
            block(n, jnp.bfloat16),
            block(n, jnp.bfloat16),
            block(n, jnp.float32),
            block(nc, jnp.float32),
            block(n, jnp.bfloat16),
            pltpu.SemaphoreType.DMA((5, most)),
            pltpu.SemaphoreType.DMA((5, most)),
        ],
        compiler_params=pltpu.CompilerParams(collective_id=0, has_side_effects=True),
    )(env_part.astype(jnp.bfloat16).reshape(n, rows, bond), parent_block, top_env.reshape(n, rows, width))


CHUNK = 8
GROUP = 8
AHEAD = 3
LINE = 4


def core_kernel(
    n, number, tens_ref, rc_ref, coef_ref, left_ref, tsel_ref, loc_ref,
    full, image, stage_t, stage_l, own_sem, csem, fsem, esem, rsem, xsem,
):
    me = lax.axis_index("shard")
    cores = n // LINE
    chip, core = me // cores, lax.rem(me, cores)
    rows = tens_ref.shape[1]
    steps = tens_ref.shape[0] // CHUNK
    other = 1 - core
    mate_chip = chip + 1 - 2 * lax.rem(chip, 2)
    twin = chip * cores + other
    mate = mate_chip * cores + core
    across = (LINE - 1 - chip) * cores + core
    far = (LINE - 1 - mate_chip) * cores + core
    middle = jnp.logical_or(chip == 1, chip == 2)
    edge = jnp.logical_or(chip == 0, chip == 3)

    barrier = pltpu.get_barrier_semaphore()
    for k in range(1, n):
        pl.semaphore_signal(
            barrier, inc=1, device_id={"shard": lax.rem(me + k, n)}, device_id_type=MESH
        )
    pl.semaphore_wait(barrier, n - 1)

    def span(q):
        return pl.ds(pl.multiple_of(q * CHUNK, CHUNK), CHUNK)

    def place(q, j):
        return full.at[span(q), pl.ds(pl.multiple_of(j * rows, rows), rows), :]

    def remote(src, dst, send, recv, j):
        return pltpu.make_async_remote_copy(
            src_ref=src, dst_ref=dst, send_sem=send, recv_sem=recv,
            device_id={"shard": j}, device_id_type=MESH,
        )

    def own_to(q, send, j):
        return remote(tens_ref.at[span(q)], place(q, me), send, rsem.at[q, me], j)

    def pass_on(q, j, send, goal):
        return remote(place(q, j), place(q, j), send, rsem.at[q, j], goal)

    def finished(which, q):
        stage, goal_ref = ((stage_t, tsel_ref), (stage_l, loc_ref))[which]
        return remote(
            stage.at[span(q)], goal_ref.at[span(q)], esem.at[which, q], xsem.at[which, q], mate
        )

    def kept(q):
        return pltpu.make_async_copy(tens_ref.at[span(q)], place(q, me), own_sem.at[q])

    def loop(count, body):
        def step(q, _):
            body(q)
            return 0

        lax.fori_loop(0, count, step, 0)

    @pl.when(edge)
    def _():
        loop(steps, lambda q: own_to(q, csem.at[0, q], mate).start())

        def take(q):
            own_to(q, csem.at[0, q], mate).wait_send()
            for which in range(2):
                finished(which, q).wait_recv()

        loop(steps, take)

    @pl.when(middle)
    def _():
        def begin(q):
            own_to(q, fsem.at[0, q], twin).start()
            kept(q).start()

        loop(steps, begin)

        def relay(q):
            own_to(q, csem.at[0, q], across).start()
            pass_on(q, mate, csem.at[1, q], twin).wait_recv()
            pass_on(q, mate, csem.at[1, q], across).start()
            pass_on(q, mate, fsem.at[1, q], twin).start()

        loop(AHEAD, relay)

        def chunk(q):
            @pl.when(q + AHEAD < steps)
            def _():
                relay(q + AHEAD)

            for slot, j in ((2, across), (3, far)):
                pass_on(q, j, fsem.at[slot, q], twin).wait_recv()
                pass_on(q, j, fsem.at[slot, q], twin).start()
            kept(q).wait()
            for slot, j in enumerate((me, mate, across, far)):
                pass_on(q, j + other - core, fsem.at[slot, q], twin).wait_recv()

            def block(g, _):
                first = q * CHUNK + g * GROUP
                for i in range(GROUP):
                    made = lax.dot_general(
                        rc_ref[...], full[first + i], (((1,), (1,)), ((), ())),
                        preferred_element_type=jnp.float32,
                    )
                    made = (made * coef_ref[...]).astype(jnp.bfloat16)
                    for t in range(number):
                        image[t, pl.ds(i * 2 * rows, 2 * rows), :] = made[
                            t * 2 * rows : (t + 1) * 2 * rows
                        ]
                    base = number * 2 * rows
                    tsel_ref[first + i] = made[base : base + rows]
                    stage_t[first + i] = made[base + rows : base + 2 * rows]
                total = jnp.dot(image[0], left_ref[0], preferred_element_type=jnp.float32)
                for t in range(1, number):
                    total += jnp.dot(image[t], left_ref[t], preferred_element_type=jnp.float32)
                total = total.astype(jnp.bfloat16).reshape(GROUP, 2 * rows, total.shape[-1])
                loc_ref[pl.ds(first, GROUP)] = total[:, :rows]
                stage_l[pl.ds(first, GROUP)] = total[:, rows:]
                return 0

            lax.fori_loop(0, CHUNK // GROUP, block, 0)
            for which in range(2):
                finished(which, q).start()

        loop(steps, chunk)

        def drain(q):
            own_to(q, fsem.at[0, q], twin).wait_send()
            own_to(q, csem.at[0, q], across).wait_send()
            pass_on(q, mate, csem.at[1, q], across).wait_send()
            for slot, j in ((1, mate), (2, across), (3, far)):
                pass_on(q, j, fsem.at[slot, q], twin).wait_send()
            for which in range(2):
                finished(which, q).wait_send()

        loop(steps, drain)


def local_of(tensor, left_ops, right_ops, weights):
    n = lax.axis_size("shard")
    me = lax.axis_index("shard")
    rows, bond = tensor.shape[0], tensor.shape[1]
    number = weights.shape[0]
    steps = bond // CHUNK
    cores = n // LINE
    chip = me // cores
    mate = (chip + 1 - 2 * (chip % 2)) * cores + me % cores
    pair = jnp.stack([me, mate])
    slabs = jnp.swapaxes(right_ops, 1, 2).reshape(number, n, rows, bond)
    chosen = slabs[:, pair]
    wanted = pair[:, None] * rows + jnp.arange(rows)[None, :]
    onehot = (wanted[:, :, None] == jnp.arange(bond)).astype(jnp.bfloat16)
    rc = jnp.concatenate([chosen, onehot[None]], axis=0).reshape((number + 1) * 2 * rows, bond)
    coef = jnp.repeat(jnp.concatenate([weights, jnp.ones((1,), jnp.float32)]), 2 * rows)[:, None]
    upward = jnp.transpose(tensor, (2, 0, 1))
    vmem = pl.BlockSpec(memory_space=pltpu.VMEM)
    hbm = pl.BlockSpec(memory_space=pl.ANY)
    slab = jax.ShapeDtypeStruct((bond, rows, bond), jnp.bfloat16)
    dma = pltpu.SemaphoreType.DMA
    return pl.pallas_call(
        functools.partial(core_kernel, n, number),
        out_shape=(slab, slab),
        in_specs=[hbm, vmem, vmem, vmem],
        out_specs=(vmem, vmem),
        scratch_shapes=[
            pltpu.VMEM((bond, bond, bond), jnp.bfloat16),
            pltpu.VMEM((number, GROUP * 2 * rows, bond), jnp.bfloat16),
            pltpu.VMEM((bond, rows, bond), jnp.bfloat16),
            pltpu.VMEM((bond, rows, bond), jnp.bfloat16),
            dma((steps,)),
            dma((2, steps)),
            dma((4, steps)),
            dma((2, steps)),
            dma((steps, n)),
            dma((2, steps)),
        ],
        compiler_params=pltpu.CompilerParams(
            collective_id=1, has_side_effects=True, vmem_limit_bytes=60 * 1024 * 1024
        ),
    )(upward, rc, coef, left_ops)


def by_exchange(tensor, left_ops, right_ops, weights):
    bond = tensor.shape[1]
    upward = lax.all_to_all(tensor, "shard", split_axis=2, concat_axis=0, tiled=True)
    regrouped = lax.all_to_all(tensor, "shard", split_axis=1, concat_axis=0, tiled=True)
    summed = jnp.zeros((bond, bond, upward.shape[2]), jnp.float32)
    for term in range(weights.shape[0]):
        image = jnp.einsum(
            "lru,rs->lsu", upward, right_ops[term], preferred_element_type=jnp.float32
        ).astype(jnp.bfloat16)
        summed = summed + weights[term] * jnp.einsum(
            "lk,lsu->ksu", left_ops[term], image, preferred_element_type=jnp.float32
        )
    local = lax.all_to_all(
        summed.astype(jnp.bfloat16), "shard", split_axis=1, concat_axis=2, tiled=True
    )
    return jnp.transpose(regrouped, (2, 1, 0)), jnp.transpose(local, (2, 1, 0))


def shards(child_tensors, leg_ops, term_ops, term_coef, parent, top_env):
    tensor = child_tensors[0]
    picks = term_ops[0]
    weights = term_coef[0]
    left_ops = leg_ops[picks[:, 0]]
    right_ops = leg_ops[picks[:, 1]]
    form = local_of if lax.axis_size("shard") == 2 * LINE else by_exchange
    slab, local = form(tensor, left_ops, right_ops, weights)
    env_part = jnp.einsum("usl,vsl->uv", slab, local, preferred_element_type=jnp.float32)
    hole = hole_of(env_part, parent[0], top_env)
    result = local.astype(jnp.float32) + jnp.einsum(
        "uv,usl->vsl", hole, slab, preferred_element_type=jnp.float32
    )
    return jnp.transpose(result.astype(jnp.bfloat16), (2, 1, 0))[None]


def solution(mesh):
    in_specs = (
        P("child", "shard", None, None),
        P(),
        P("child", None, None),
        P("child", None),
        P("child", "shard", None),
        P(),
    )
    out_specs = P("child", None, "shard", None)
    return jax.shard_map(shards, mesh=mesh, in_specs=in_specs, out_specs=out_specs, check_vma=False)
```
